32 devices in a mesh: group: 2 (over x), lev: 2 (over core), row: 8 (over z, y).
Axes of the slice: x: 2, y: 2, z: 4, core: 2. Of those that a mesh axis runs over, the one named last changes fastest.
Arguments:
- fields: bfloat16 [6, 90, 64, 1024], P('group', 'lev', 'row'), parts along dimension 0, may hold values from -6 to 6
- vertical_modes: bfloat16 [8, 90, 64, 1024], P(None, 'lev', 'row'), may hold values from -0.625 to 0.625
- diffusivity: float32 [64, 1024], P('row'), may hold values from 0.05 to 0.245
- land_mask: int32 [64, 1024], P('row'), may hold values 0 or 1
- wet_levels: int32 [64, 1024], P('row'), may hold values from 1 to 90
Outputs:
- filtered: bfloat16 [6, 90, 64, 1024], P('group', 'lev', 'row'), parts along dimension 0
- modal_flux: float32 [6, 8, 64, 1024], P('group', None, 'row', 'lev'), parts along dimension 0
The draws below stay inside these ranges and needn't reach their ends.
There are 2 independent parts, one for each index of `group`. The reference program is written for one: setup_inputs(seed, part) draws one part's arguments, and reference() takes and returns one part's arrays. A program takes and returns all parts, laid end to end along the dimension named above; an argument that names none is the same for every part. Nothing has to cross between parts.
All inputs are finite; a program needn't handle non-finite values. No bound on the sum of `land_mask` on one device may be relied on, other than what follows from the above.
Results may differ from the reference program's by a relative error of at most 0.00092.
Values may be sent and summed in bfloat16 or wider, within the bound.
No kernel may reach another device: no remote copies, remote signals or barrier semaphores. Data moves between devices by JAX's collectives and lax.ppermute only.
A program may use at most 192 MiB of HBM per device.

```python
import math
import jax
import jax.numpy as jnp
from jax import lax

L = 90
K = 8
NX = 1024
ITERS = 10
NY = 64


def plant(array, stream_key, least, top_value):
    longest = array.shape.index(max(array.shape))
    spots = []
    for shift in (0, 1):
        where = [jax.random.randint(jax.random.fold_in(stream_key, axis), (), 0, length) for axis, length in enumerate(array.shape)]
        where[longest] = (where[longest] + shift) % array.shape[longest]
        spots.append(tuple(where))
    return array.at[spots[0]].set(least).at[spots[1]].set(top_value)


def steps_of(stream_key, extent, split, low, largest):
    gain = 1.0
    for dim, blocks in split:
        steps = jax.random.uniform(jax.random.fold_in(jax.random.fold_in(stream_key, 6), dim), (blocks,), jnp.float32, low / len(split), largest / len(split))
        gain = gain * jnp.repeat(jnp.exp(steps), extent[dim] // blocks).reshape((-1,) + (1,) * (len(extent) - 1 - dim))
    return gain


def gaussian(own_key, dims, deviation, limit, shards=(), kind=jnp.bfloat16):
    entries = jax.random.normal(own_key, dims, jnp.float32) * deviation
    if len(shards) > 0:
        entries = steps_of(own_key, dims, shards, -0.22, 0.18) * entries
    return jnp.clip(entries, min=-limit, max=limit).astype(kind)


def setup_inputs(seed: int = 0, part: int = 0) -> dict:
    key_list = jax.random.split(jax.random.key(seed), 6)
    part_splits = jax.random.split(jax.random.fold_in(key_list[5], part), 6)
    return {
        "fields": gaussian(part_splits[0], (3, L, NY, NX), 1.0, 6.0, ((1, 2), (2, 8))),
        "vertical_modes": gaussian(key_list[1], (K, L, NY, NX), L ** -0.5, 0.625, ((1, 2), (2, 8))),
        "diffusivity": jnp.clip(jnp.exp(math.log(0.245) - 1.5892352 * jax.random.uniform(key_list[2], (NY, NX), jnp.float32) ** steps_of(key_list[2], (NY, NX), ((0, 8),), -0.2, 0.2)), 0.05, 0.245),
        "land_mask": plant((jax.random.randint(key_list[3], (NY, NX), 0, 10) < 9).astype(jnp.int32), jax.random.fold_in(key_list[3], 1), 0, 1),
        "wet_levels": plant(jax.random.randint(key_list[4], (NY, NX), 1, L + 1), jax.random.fold_in(key_list[4], 1), 1, L).astype(jnp.int32),
    }


def reference(fields, vertical_modes, diffusivity, land_mask, wet_levels):
    level_index = jnp.arange(L, dtype=jnp.int32)
    wet_cells = ((land_mask[None] == 1) & (level_index[:, None, None] < wet_levels[None])).astype(jnp.float32)
    east_weight = 0.5 * (diffusivity[:, :-1] + diffusivity[:, 1:])[None] * wet_cells[:, :, :-1] * wet_cells[:, :, 1:]
    north_weight = 0.5 * (diffusivity[:-1] + diffusivity[1:])[None] * wet_cells[:, :-1] * wet_cells[:, 1:]
    current = fields.astype(jnp.float32)
    for step_index in range(ITERS):
        east_flux = east_weight * (current[..., 1:] - current[..., :-1])
        north_flux = north_weight * (current[..., 1:, :] - current[..., :-1, :])
        east_side = jnp.pad(east_flux, ((0, 0), (0, 0), (0, 0), (0, 1))) - jnp.pad(east_flux, ((0, 0), (0, 0), (0, 0), (1, 0)))
        north_side = jnp.pad(north_flux, ((0, 0), (0, 0), (0, 1), (0, 0))) - jnp.pad(north_flux, ((0, 0), (0, 0), (1, 0), (0, 0)))
        current = current + east_side + north_side
    filtered = current.astype(jnp.bfloat16)
    modes_wide = vertical_modes.astype(jnp.float32)
    rounded_wide = filtered.astype(jnp.float32)
    amplitude = jnp.stack([jnp.einsum("klyx,lyx->kyx", modes_wide, rounded_wide[field_index], precision=lax.Precision.HIGHEST) for field_index in range(3)])
    modal_flux = jnp.stack([amplitude[0] * amplitude[2], amplitude[1] * amplitude[2], 0.5 * (amplitude[0] * amplitude[0] + amplitude[1] * amplitude[1])])
    return filtered, modal_flux
```

```python
import jax
import jax.numpy as jnp
from jax import lax
from jax.experimental import pallas as pl
from jax.experimental.pallas import tpu as pltpu
from jax.sharding import PartitionSpec as P

ITERS = 10
TURN_COST = 20
GATHER_COST = 20
FILTER_COST = 1
PROJECT_COST = 20
GROUP = 8
LANES = 128
PLANES = 4
F32 = jnp.float32
BF16 = jnp.bfloat16


def whole(space=pltpu.VMEM):
    return pl.BlockSpec(memory_space=space)


def call(body, landed=(), **kw):
    shapes = tuple(pltpu.HBM(a.shape, a.dtype) for a in kw.pop("out_shape"))
    inner = pl.pallas_call(body, out_shape=shapes, **kw)

    def run(*args):
        pinned = []
        for i, (arg, spec) in enumerate(zip(args, kw["in_specs"])):
            if spec.memory_space != pltpu.SMEM:
                space = pltpu.VMEM if i in landed else pltpu.HBM
                arg = pltpu.with_memory_space_constraint(arg, space)
            pinned.append(arg)
        return inner(*pinned)

    return run


def params(mib):
    return pltpu.CompilerParams(vmem_limit_bytes=mib * 1024 * 1024)


def cost(us):
    return pl.CostEstimate(flops=0, transcendentals=0, bytes_accessed=us * 3_690_000)


def spread_fill(spread_ref, unspread_ref):
    cols = spread_ref.shape[0]
    tiles = cols // LANES
    for first in range(0, cols, LANES):
        here = first + lax.broadcasted_iota(jnp.int32, (LANES, cols), 0)
        there = lax.broadcasted_iota(jnp.int32, (LANES, cols), 1)
        rows = pl.ds(first, LANES)
        to_spot = here == (there % LANES) * tiles + there // LANES
        to_col = there == (here % LANES) * tiles + here // LANES
        spread_ref[rows, :] = jnp.where(to_spot, 1.0, 0.0).astype(BF16)
        unspread_ref[rows, :] = jnp.where(to_col, 1.0, 0.0).astype(BF16)


def turn_piece(piece, spread_ref, turn_ref, put, put_statics=None):
    count, rows, cols = piece.shape
    flat = piece.astype(F32).reshape(count * rows, cols).astype(BF16)
    moved = jnp.dot(flat, spread_ref[...], preferred_element_type=F32)
    fields = count // GROUP
    for j in range(cols // LANES):
        turn_ref[j, pl.ds(0, count * rows), :] = moved[:, j * LANES : (j + 1) * LANES]
    for j in range(cols // LANES):
        lanes = pl.ds(j * LANES, LANES)
        for r in range(rows):
            for f in range(fields):
                value = turn_ref[j, pl.ds(f * GROUP * rows + r, GROUP, stride=rows), :]
                put(r, f, fields, lanes, value.astype(BF16))
            if put_statics is not None:
                first = fields * GROUP * rows + r
                put_statics(r, lanes, turn_ref[j, pl.ds(first, PLANES, stride=rows), :])


def turn_body(base_ref, fields_ref, planes_ref, spread_ref, unspread_ref, statics_ref, *refs):
    buf_ref, turn_ref, sems = refs[-3:]
    outs = refs[:-3]
    _, fields, _, rows, cols = buf_ref.shape
    copies = [
        pltpu.make_async_copy(
            fields_ref.at[:, pl.ds(base_ref[n], GROUP)], buf_ref.at[n], sems.at[n]
        )
        for n in range(len(outs))
    ]
    for copy in copies:
        copy.start()
    spread_fill(spread_ref, unspread_ref)
    for n, out in enumerate(outs):
        copies[n].wait()

        def put(r, f, count, lanes, value):
            out[r * count + f, :, lanes] = value

        def put_statics(r, lanes, value):
            at = r * PLANES
            statics_ref[at // GROUP, pl.ds(at % GROUP, PLANES), lanes] = value

        piece = buf_ref[n].reshape(fields * GROUP, rows, cols)
        if n == 0:
            piece = jnp.concatenate([piece, planes_ref[...]], axis=0)
        turn_piece(piece, spread_ref, turn_ref, put, put_statics if n == 0 else None)


def turn(bases, fields, planes):
    count, _, rows, cols = fields.shape
    out = jax.ShapeDtypeStruct((rows * count, GROUP, cols), BF16)
    square = jax.ShapeDtypeStruct((cols, cols), BF16)
    many = len(bases)
    return call(
        turn_body,
        out_shape=(square, square, jax.ShapeDtypeStruct((rows * PLANES // GROUP, GROUP, cols), F32))
        + (out,) * many,
        in_specs=[whole(pltpu.SMEM), whole(pl.ANY), whole()],
        out_specs=(whole(),) * (3 + many),
        scratch_shapes=[
            pltpu.VMEM((many, count, GROUP, rows, cols), BF16),
            pltpu.VMEM((cols // LANES, (count * GROUP + PLANES) * rows, LANES), F32),
            pltpu.SemaphoreType.DMA((many,)),
        ],
        compiler_params=params(16),
        cost_estimate=cost(TURN_COST),
        name="turn",
    )(jnp.stack(bases), fields, planes)


def gather_body(where_ref, own_ref, part_ref, spread_ref, *refs):
    refs = list(refs)
    own_statics_ref = refs.pop(0) if len(refs) > 4 else None
    pair_ref, first_ref, second_ref, turn_ref = refs[:4]
    statics_ref = refs[4] if own_statics_ref is not None else None
    rows = part_ref.shape[1]
    fields = own_ref.shape[0] // rows
    side, odd = (where_ref[0], where_ref[1])
    own_start = side * rows
    part_start = rows - own_start
    for r in range(rows * fields):
        pair_ref[own_start * fields + r] = own_ref[r]

    def put(r, f, count, lanes, value):
        pair_ref[(part_start + r) * count + f, :, lanes] = value

    put_statics = None
    if statics_ref is not None:
        tiles = rows * PLANES // GROUP
        statics_ref[pl.ds(side * tiles, tiles)] = own_statics_ref[...]

        def put_statics(r, lanes, value):
            at = r * PLANES
            base = (1 - side) * tiles + at // GROUP
            statics_ref[base, pl.ds(at % GROUP, PLANES), lanes] = value

    turn_piece(part_ref[...], spread_ref, turn_ref, put, put_statics)
    tail = 2 * rows - ITERS
    for dst, pick in ((first_ref, 1 - odd), (second_ref, odd)):
        for r in range(ITERS * fields):
            dst[r] = pair_ref[pick * tail * fields + r]
        if statics_ref is not None:
            count = ITERS * PLANES // GROUP
            value = statics_ref[pl.ds(pick * (tail * PLANES // GROUP), count)]
            dst[pl.ds(ITERS * fields, count)] = value.astype(BF16)
    if statics_ref is not None:
        pair_ref[pl.ds(2 * rows * fields, statics_ref.shape[0])] = statics_ref[...].astype(BF16)


def gather_rows(where, own, part, spread, statics=None):
    count, rows, cols = part.shape
    fields = own.shape[0] // rows
    extra = 0 if statics is None else PLANES

    def out(n):
        return jax.ShapeDtypeStruct((n * fields + n * extra // GROUP, GROUP, cols), BF16)

    scratch = [pltpu.VMEM((cols // LANES, count * rows, LANES), F32)]
    if statics is not None:
        scratch.append(pltpu.VMEM((2 * rows * PLANES // GROUP, GROUP, cols), F32))
    args = (where, own, part, spread) + (() if statics is None else (statics,))
    return call(
        gather_body,
        landed=(2,),
        out_shape=(out(2 * rows), out(ITERS), out(ITERS)),
        in_specs=[whole(pltpu.SMEM)] + [whole()] * (len(args) - 1),
        out_specs=(whole(),) * 3,
        scratch_shapes=scratch,
        compiler_params=params(16),
        cost_estimate=cost(GATHER_COST),
        name="gather_rows",
    )(*args)


def make_faces(face_ref, planes_ref, spare_ref):
    _, tiles, total, _ = face_ref.shape
    spare_ref[...] = jnp.zeros(spare_ref.shape, F32)

    def plane(j, p):
        return planes_ref[j, pl.ds(p, total, stride=PLANES), :]

    for j in range(tiles):
        spare_ref[0, j, pl.ds(0, total), :] = plane(j, 0) + plane(j, 1) + plane(j, 2)
        spare_ref[1, j, pl.ds(0, total), :] = plane(j, 3)
    lane = lax.broadcasted_iota(jnp.int32, (total, LANES), 1)
    for j in range(tiles):
        here, east, north = ([], [], [])
        for i in range(2):
            here.append(spare_ref[i, j, pl.ds(0, total), :])
            if j + 1 < tiles:
                east.append(spare_ref[i, j + 1, pl.ds(0, total), :])
            else:
                east.append(pltpu.roll(spare_ref[i, 0], LANES - 1, 1)[:total])
            north.append(spare_ref[i, j, pl.ds(1, total), :])
        wet_east = jnp.minimum(here[1], east[1])
        if j + 1 == tiles:
            wet_east = jnp.where(lane == LANES - 1, 0.0, wet_east)
        face_ref[0, j] = 0.5 * (here[0] + east[0])
        face_ref[1, j] = wet_east
        face_ref[2, j] = 0.5 * (here[0] + north[0])
        face_ref[3, j] = jnp.minimum(here[1], north[1])


def filter_body(leads, scal_ref, pair_ref, first_ref, second_ref, back_ref, *refs):
    face_ref, mine_ref, send_ref = refs[:3]
    cur_ref, east_ref, west_ref, north_ref, turn_ref = refs[3:8]
    fields, total, tiles, _, _ = cur_ref.shape
    cols = tiles * LANES
    pair = total - 2 * ITERS
    rows = pair // 2
    side = scal_ref[0]
    level = (scal_ref[2] + lax.broadcasted_iota(jnp.int32, (GROUP, LANES), 0)).astype(F32)

    def fill(src, dst_row, count):
        for r in range(count):
            for f in range(fields):
                for j in range(tiles):
                    value = src[r * fields + f, :, pl.ds(j * LANES, LANES)]
                    cur_ref[f, dst_row + r, j] = value.astype(F32)
        if leads:
            planes_ref = refs[8]
            block = count * PLANES
            for j in range(tiles):
                value = src[pl.ds(count * fields, block // GROUP), :, pl.ds(j * LANES, LANES)]
                planes_ref[j, pl.ds(dst_row * PLANES, block), :] = value.astype(F32).reshape(
                    block, LANES
                )

    @pl.when(scal_ref[1] == 0)
    def _():
        fill(second_ref, 0, ITERS)
        fill(first_ref, ITERS + pair, ITERS)

    @pl.when(scal_ref[1] == 1)
    def _():
        fill(first_ref, 0, ITERS)
        fill(second_ref, ITERS + pair, ITERS)

    fill(pair_ref, ITERS, pair)
    if leads:
        make_faces(face_ref, refs[8], refs[9])

    def weights(r, _):
        for j in range(tiles):

            def spread(i):
                return jnp.broadcast_to(face_ref[i, j, pl.ds(r, 1), :], (GROUP, LANES))

            east = jnp.where(level < spread(1), spread(0), 0.0)
            east_ref[r, j] = east
            north_ref[r, j] = jnp.where(level < spread(3), spread(2), 0.0)
        west_ref[r] = pltpu.roll(east, 1, 1)
        return 0

    lax.fori_loop(0, total, weights, 0, unroll=4)

    def one_field(f, _):
        for step in range(1, ITERS + 1):
            here = [cur_ref[f, step, j] for j in range(tiles)]
            south = [
                north_ref[step - 1, j] * (here[j] - cur_ref[f, step - 1, j]) for j in range(tiles)
            ]
            first = pltpu.roll(here[0], LANES - 1, 1)
            last = pltpu.roll(here[-1], 1, 1)
            for r in range(step, total - step):
                ahead = [cur_ref[f, r + 1, j] for j in range(tiles)]
                flux = west_ref[r] * (here[0] - last)
                for j in range(tiles):
                    beyond = here[j + 1] if j + 1 < tiles else first
                    east = east_ref[r, j] * (beyond - here[j])
                    north = north_ref[r, j] * (ahead[j] - here[j])
                    cur_ref[f, r, j] = here[j] + (east - flux) + (north - south[j])
                    flux = east
                    south[j] = north
                first = pltpu.roll(ahead[0], LANES - 1, 1)
                last = pltpu.roll(ahead[-1], 1, 1)
                here = ahead
        return 0

    lax.fori_loop(0, fields, one_field, 0)

    def emit(dst, start):
        for f in range(fields):
            for r in range(rows):
                for j in range(tiles):
                    spots = pl.ds(f * GROUP * rows + r, GROUP, stride=rows)
                    turn_ref[j, spots, :] = cur_ref[f, start + r, j]
        flat = jnp.concatenate([turn_ref[j].astype(BF16) for j in range(tiles)], axis=1)
        moved = jnp.dot(flat, back_ref[...], preferred_element_type=F32)
        dst[...] = moved.reshape(fields, GROUP, rows, cols).astype(BF16)

    emit(send_ref, ITERS + rows * (1 - side))
    emit(mine_ref, ITERS + rows * side)


def filter_rows(scalars, pair, first, second, unspread, faces, fields, rows):
    cols = pair.shape[2]
    total = 2 * rows + 2 * ITERS
    tiles = cols // LANES
    leads = faces is None
    out = jax.ShapeDtypeStruct((fields, GROUP, rows, cols), BF16)
    face = jax.ShapeDtypeStruct((4, tiles, total, LANES), F32)
    scratch = [
        pltpu.VMEM((fields, total, tiles, GROUP, LANES), F32),
        pltpu.VMEM((total, tiles, GROUP, LANES), F32),
        pltpu.VMEM((total, GROUP, LANES), F32),
        pltpu.VMEM((total, tiles, GROUP, LANES), F32),
        pltpu.VMEM((tiles, fields * GROUP * rows, LANES), F32),
    ]
    if leads:
        spare = -(-(total + 1) // GROUP) * GROUP
        scratch += [
            pltpu.VMEM((tiles, total * PLANES, LANES), F32),
            pltpu.VMEM((2, tiles, spare, LANES), F32),
        ]

    def body(*refs):
        filter_body(leads, *refs)

    return call(
        body,
        landed=(2, 3),
        out_shape=((face,) if leads else ()) + (out, out),
        in_specs=[whole(pltpu.SMEM)]
        + [whole()] * 4
        + ([] if leads else [whole()]),
        out_specs=(whole(),) * (3 if leads else 2),
        scratch_shapes=scratch,
        compiler_params=params(24),
        cost_estimate=cost(FILTER_COST),
        name="filter_rows",
    )(scalars, pair, first, second, unspread, *(() if leads else (faces,)))


def project_body(takes, halves, has_start, base_ref, *refs):
    count = len(takes)
    refs = list(refs)
    chunk_refs = refs[:count]
    refs = refs[count:]
    modes_ref = refs.pop(0)
    start_ref = None
    if has_start:
        start_ref = refs.pop(0)
        refs.pop(0)
    out_ref = refs.pop(0)
    keep_ref = give_ref = amp_ref = None
    if halves > 1:
        keep_ref, give_ref = (refs.pop(0), refs.pop(0))
    else:
        amp_ref = refs.pop(0)
    mode_bufs = refs[:count]
    out_sems, mode_sems = refs[count:]
    fields, _, rows, cols = chunk_refs[0].shape
    modes = modes_ref.shape[0]
    fetches = [
        pltpu.make_async_copy(
            modes_ref.at[:, pl.ds(base_ref[n, 0], takes[n])], mode_bufs[n], mode_sems.at[n]
        )
        for n in range(count)
    ]
    copies = [
        pltpu.make_async_copy(
            chunk_refs[n].at[:, pl.ds(base_ref[n, 1], takes[n])],
            out_ref.at[:, pl.ds(base_ref[n, 0], takes[n])],
            out_sems.at[n],
        )
        for n in range(count)
    ]
    for fetch in fetches:
        fetch.start()
    for copy in copies:
        copy.start()
    for n in range(count):
        fetches[n].wait()

        def one_tile(tile, dst, dst_tile, _):
            lanes = pl.ds(pl.multiple_of(tile * LANES, LANES), LANES)
            into = pl.ds(pl.multiple_of(dst_tile * LANES, LANES), LANES)
            sums = []
            for f in range(fields):
                for k in range(modes):
                    if n > 0:
                        sums.append(amp_ref[f, k, :, lanes])
                    elif has_start:
                        sums.append(start_ref[f, k, :, lanes])
                    else:
                        sums.append(jnp.zeros((rows, LANES), F32))
            for i in range(takes[n]):
                values = [
                    chunk_refs[n][f, base_ref[n, 1] + i, :, lanes].astype(F32)
                    for f in range(fields)
                ]
                for k in range(modes):
                    mode = mode_bufs[n][k, i, :, lanes].astype(F32)
                    for f in range(fields):
                        sums[f * modes + k] = sums[f * modes + k] + mode * values[f]
            for f in range(fields):
                for k in range(modes):
                    dst[f, k, :, into] = sums[f * modes + k]
            return 0

        tiles = cols // LANES
        if halves == 1:
            lax.fori_loop(0, tiles, lambda i, z: one_tile(i, amp_ref, i, z), 0)
        else:
            width = tiles // halves
            mine = base_ref[n, 2] * width
            rest = (1 - base_ref[n, 2]) * width
            lax.fori_loop(0, width, lambda i, z: one_tile(rest + i, give_ref, i, z), 0)
            lax.fori_loop(0, width, lambda i, z: one_tile(mine + i, keep_ref, i, z), 0)
    for copy in copies:
        copy.wait()


def project(bases, chunks, takes, vertical_modes, levels, halves, carried=()):
    count = len(chunks)
    fields, _, rows, cols = chunks[0].shape
    modes = vertical_modes.shape[0]

    def body(*refs):
        project_body(takes, halves, bool(carried), *refs)

    amplitude = jax.ShapeDtypeStruct((fields, modes, rows, cols // halves), F32)

    return call(
        body,
        landed=(1,) if carried else (),
        out_shape=(jax.ShapeDtypeStruct((fields, levels, rows, cols), BF16),)
        + (amplitude,) * halves,
        in_specs=[whole(pltpu.SMEM)]
        + [whole()] * count
        + [whole(pl.ANY)]
        + ([whole(), whole(pl.ANY)] if carried else []),
        out_specs=(whole(pl.ANY),) + (whole(),) * halves,
        input_output_aliases={count + 3: 0} if carried else {},
        scratch_shapes=[pltpu.VMEM((modes, take, rows, cols), BF16) for take in takes]
        + [pltpu.SemaphoreType.DMA((count,))] * 2,
        compiler_params=params(24),
        cost_estimate=cost(PROJECT_COST),
        name="project",
    )(bases, *chunks, vertical_modes, *carried)


def flux_body(keep_ref, other_ref, out_ref):
    total = keep_ref[...] + other_ref[...]
    out_ref[0] = total[0] * total[2]
    out_ref[1] = total[1] * total[2]
    out_ref[2] = 0.5 * (total[0] * total[0] + total[1] * total[1])


def statics_planes(diffusivity, depth):
    high = lax.reduce_precision(diffusivity, 8, 7)
    middle = lax.reduce_precision(diffusivity - high, 8, 7)
    low = diffusivity - high - middle
    return jnp.stack([high, middle, low, depth]).astype(BF16)


def per_device(fields, vertical_modes, diffusivity, land_mask, wet_levels):
    count, levels, rows, cols = fields.shape
    size = lax.axis_size("row")
    row = lax.axis_index("row")
    lev = lax.axis_index("lev")
    side = row % 2
    pairs = [(i, i ^ 1) for i in range(size)]
    odd = (row // 2) % 2
    near = [(i, i ^ 2) for i in range(size)]
    far = [(i, ((i + 2) ^ 2) - 2) for i in range(2, size - 2)]
    chunks = -(-(-(-levels // 2)) // GROUP)

    def base(c, which):
        return jnp.where(which == 0, GROUP * c, levels - GROUP * (c + 1)).astype(jnp.int32)

    theirs = [base(c, 1 - side) for c in range(chunks)]
    ours = [base(c, side) for c in range(chunks)]
    depth = (land_mask * wet_levels).astype(F32)
    planes = statics_planes(diffusivity, depth)
    parts = []
    for c, b in enumerate(theirs):
        piece = lax.dynamic_slice_in_dim(fields, b, GROUP, 1)
        piece = piece.reshape(count * GROUP, rows, cols)
        if c == 0:
            piece = jnp.concatenate([piece, planes], axis=0)
        parts.append(lax.ppermute(piece, "row", pairs))
    spread, unspread, statics, *owns = turn(ours, fields, planes)

    where = jnp.stack([side, odd])
    mine, returned, edges = ([], [], [])
    faces = None
    for c in range(chunks):
        part = parts[c]
        if c > 0:
            part, *_ = lax.optimization_barrier((part, edges[-1], mine[: c - 1]))
        pair, first, second = gather_rows(
            where, owns[c], part, spread, statics if c == 0 else None
        )
        edges.append(first)
        first = lax.ppermute(first, "row", near)
        second = lax.ppermute(second, "row", far)
        if c > 0:
            first, *_ = lax.optimization_barrier((first, mine[-1], returned[: c - 1]))
        scalars = jnp.stack([side, odd, lev * levels + ours[c]])
        *lead, kept, sent = filter_rows(
            scalars, pair, first, second, unspread, faces, count, rows
        )
        if c == 0:
            faces = lead[0]
        mine.append(kept)
        returned.append(lax.ppermute(sent, "row", pairs))

    cut = levels - (2 * chunks - 1) * GROUP
    first = jnp.where(side == 0, GROUP - cut, 0).astype(jnp.int32)
    zero = jnp.zeros((), jnp.int32)
    bases = [jnp.stack([b, zero]) for b in ours + theirs[:-1]]
    filtered, amplitude = project(
        jnp.stack(bases),
        mine + returned[:-1],
        [GROUP] * (2 * chunks - 1),
        vertical_modes,
        levels,
        1,
    )
    filtered, keep, give = project(
        jnp.stack([theirs[-1] + first, first, lev])[None],
        returned[-1:],
        [cut],
        vertical_modes,
        levels,
        lax.axis_size("lev"),
        (amplitude, filtered),
    )
    other = lax.ppermute(give, "lev", [(0, 1), (1, 0)])
    modal_flux = pl.pallas_call(
        flux_body, out_shape=jax.ShapeDtypeStruct(keep.shape, F32), name="flux"
    )(keep, other)
    return (filtered, modal_flux)


def solution(mesh):
    placed = (
        P("group", "lev", "row", None),
        P(None, "lev", "row", None),
        P("row", None),
        P("row", None),
        P("row", None),
    )
    return jax.shard_map(
        per_device,
        mesh=mesh,
        in_specs=placed,
        out_specs=(P("group", "lev", "row", None), P("group", None, "row", "lev")),
        check_vma=False,
    )
```

```python
import jax
import jax.numpy as jnp
from jax import lax
from jax.experimental import pallas as pl
from jax.experimental.pallas import tpu as pltpu
from jax.sharding import PartitionSpec as P

ITERS = 10
TURN_COST = 20
GATHER_COST = 20
FILTER_COST = 1
PROJECT_COST = 20
GROUP = 8
LANES = 128
PLANES = 4
F32 = jnp.float32
BF16 = jnp.bfloat16


def whole(space=pltpu.VMEM):
    return pl.BlockSpec(memory_space=space)


def call(body, landed=(), **kw):
    shapes = tuple(pltpu.HBM(a.shape, a.dtype) for a in kw.pop("out_shape"))
    inner = pl.pallas_call(body, out_shape=shapes, **kw)

    def run(*args):
        pinned = []
        for i, (arg, spec) in enumerate(zip(args, kw["in_specs"])):
            if spec.memory_space != pltpu.SMEM:
                space = pltpu.VMEM if i in landed else pltpu.HBM
                arg = pltpu.with_memory_space_constraint(arg, space)
            pinned.append(arg)
        return inner(*pinned)

    return run


def params(mib):
    return pltpu.CompilerParams(vmem_limit_bytes=mib * 1024 * 1024)


def cost(us):
    return pl.CostEstimate(flops=us * 1_150_000_000, transcendentals=0, bytes_accessed=us * 3_690_000)


def spread_fill(spread_ref, unspread_ref):
    cols = spread_ref.shape[0]
    tiles = cols // LANES
    for first in range(0, cols, LANES):
        here = first + lax.broadcasted_iota(jnp.int32, (LANES, cols), 0)
        there = lax.broadcasted_iota(jnp.int32, (LANES, cols), 1)
        rows = pl.ds(first, LANES)
        to_spot = here == (there % LANES) * tiles + there // LANES
        to_col = there == (here % LANES) * tiles + here // LANES
        spread_ref[rows, :] = jnp.where(to_spot, 1.0, 0.0).astype(BF16)
        unspread_ref[rows, :] = jnp.where(to_col, 1.0, 0.0).astype(BF16)


def turn_piece(piece, spread_ref, turn_ref, put, put_statics=None):
    count, rows, cols = piece.shape
    flat = piece.astype(F32).reshape(count * rows, cols).astype(BF16)
    moved = jnp.dot(flat, spread_ref[...], preferred_element_type=F32)
    fields = count // GROUP
    for j in range(cols // LANES):
        turn_ref[j, pl.ds(0, count * rows), :] = moved[:, j * LANES : (j + 1) * LANES]
    for j in range(cols // LANES):
        lanes = pl.ds(j * LANES, LANES)
        for r in range(rows):
            for f in range(fields):
                value = turn_ref[j, pl.ds(f * GROUP * rows + r, GROUP, stride=rows), :]
                put(r, f, fields, lanes, value.astype(BF16))
            if put_statics is not None:
                first = fields * GROUP * rows + r
                put_statics(r, lanes, turn_ref[j, pl.ds(first, PLANES, stride=rows), :])


def turn_body(base_ref, fields_ref, planes_ref, spread_ref, unspread_ref, statics_ref, *refs):
    buf_ref, turn_ref, sems = refs[-3:]
    outs = refs[:-3]
    _, fields, _, rows, cols = buf_ref.shape
    copies = [
        pltpu.make_async_copy(
            fields_ref.at[:, pl.ds(base_ref[n], GROUP)], buf_ref.at[n], sems.at[n]
        )
        for n in range(len(outs))
    ]
    for copy in copies:
        copy.start()
    spread_fill(spread_ref, unspread_ref)
    for n, out in enumerate(outs):
        copies[n].wait()

        def put(r, f, count, lanes, value):
            out[r * count + f, :, lanes] = value

        def put_statics(r, lanes, value):
            at = r * PLANES
            statics_ref[at // GROUP, pl.ds(at % GROUP, PLANES), lanes] = value

        piece = buf_ref[n].reshape(fields * GROUP, rows, cols)
        if n == 0:
            piece = jnp.concatenate([piece, planes_ref[...]], axis=0)
        turn_piece(piece, spread_ref, turn_ref, put, put_statics if n == 0 else None)


def turn(bases, fields, planes):
    count, _, rows, cols = fields.shape
    out = jax.ShapeDtypeStruct((rows * count, GROUP, cols), BF16)
    square = jax.ShapeDtypeStruct((cols, cols), BF16)
    many = len(bases)
    return call(
        turn_body,
        out_shape=(square, square, jax.ShapeDtypeStruct((rows * PLANES // GROUP, GROUP, cols), F32))
        + (out,) * many,
        in_specs=[whole(pltpu.SMEM), whole(pl.ANY), whole()],
        out_specs=(whole(),) * (3 + many),
        scratch_shapes=[
            pltpu.VMEM((many, count, GROUP, rows, cols), BF16),
            pltpu.VMEM((cols // LANES, (count * GROUP + PLANES) * rows, LANES), F32),
            pltpu.SemaphoreType.DMA((many,)),
        ],
        compiler_params=params(16),
        cost_estimate=cost(TURN_COST),
        name="turn",
    )(jnp.stack(bases), fields, planes)


def gather_body(where_ref, own_ref, part_ref, spread_ref, *refs):
    refs = list(refs)
    own_statics_ref = refs.pop(0) if len(refs) > 4 else None
    pair_ref, first_ref, second_ref, turn_ref = refs[:4]
    statics_ref = refs[4] if own_statics_ref is not None else None
    rows = part_ref.shape[1]
    fields = own_ref.shape[0] // rows
    side, odd = (where_ref[0], where_ref[1])
    own_start = side * rows
    part_start = rows - own_start
    for r in range(rows * fields):
        pair_ref[own_start * fields + r] = own_ref[r]

    def put(r, f, count, lanes, value):
        pair_ref[(part_start + r) * count + f, :, lanes] = value

    put_statics = None
    if statics_ref is not None:
        tiles = rows * PLANES // GROUP
        statics_ref[pl.ds(side * tiles, tiles)] = own_statics_ref[...]

        def put_statics(r, lanes, value):
            at = r * PLANES
            base = (1 - side) * tiles + at // GROUP
            statics_ref[base, pl.ds(at % GROUP, PLANES), lanes] = value

    turn_piece(part_ref[...], spread_ref, turn_ref, put, put_statics)
    tail = 2 * rows - ITERS
    for dst, pick in ((first_ref, 1 - odd), (second_ref, odd)):
        for r in range(ITERS * fields):
            dst[r] = pair_ref[pick * tail * fields + r]
        if statics_ref is not None:
            count = ITERS * PLANES // GROUP
            value = statics_ref[pl.ds(pick * (tail * PLANES // GROUP), count)]
            dst[pl.ds(ITERS * fields, count)] = value.astype(BF16)
    if statics_ref is not None:
        pair_ref[pl.ds(2 * rows * fields, statics_ref.shape[0])] = statics_ref[...].astype(BF16)


def gather_rows(where, own, part, spread, statics=None):
    count, rows, cols = part.shape
    fields = own.shape[0] // rows
    extra = 0 if statics is None else PLANES

    def out(n):
        return jax.ShapeDtypeStruct((n * fields + n * extra // GROUP, GROUP, cols), BF16)

    scratch = [pltpu.VMEM((cols // LANES, count * rows, LANES), F32)]
    if statics is not None:
        scratch.append(pltpu.VMEM((2 * rows * PLANES // GROUP, GROUP, cols), F32))
    args = (where, own, part, spread) + (() if statics is None else (statics,))
    return call(
        gather_body,
        landed=(2,),
        out_shape=(out(2 * rows), out(ITERS), out(ITERS)),
        in_specs=[whole(pltpu.SMEM)] + [whole()] * (len(args) - 1),
        out_specs=(whole(),) * 3,
        scratch_shapes=scratch,
        compiler_params=params(16),
        cost_estimate=cost(GATHER_COST),
        name="gather_rows",
    )(*args)


def make_faces(face_ref, planes_ref, spare_ref):
    _, tiles, total, _ = face_ref.shape
    spare_ref[...] = jnp.zeros(spare_ref.shape, F32)

    def plane(j, p):
        return planes_ref[j, pl.ds(p, total, stride=PLANES), :]

    for j in range(tiles):
        spare_ref[0, j, pl.ds(0, total), :] = plane(j, 0) + plane(j, 1) + plane(j, 2)
        spare_ref[1, j, pl.ds(0, total), :] = plane(j, 3)
    lane = lax.broadcasted_iota(jnp.int32, (total, LANES), 1)
    for j in range(tiles):
        here, east, north = ([], [], [])
        for i in range(2):
            here.append(spare_ref[i, j, pl.ds(0, total), :])
            if j + 1 < tiles:
                east.append(spare_ref[i, j + 1, pl.ds(0, total), :])
            else:
                east.append(pltpu.roll(spare_ref[i, 0], LANES - 1, 1)[:total])
            north.append(spare_ref[i, j, pl.ds(1, total), :])
        wet_east = jnp.minimum(here[1], east[1])
        if j + 1 == tiles:
            wet_east = jnp.where(lane == LANES - 1, 0.0, wet_east)
        face_ref[0, j] = 0.5 * (here[0] + east[0])
        face_ref[1, j] = wet_east
        face_ref[2, j] = 0.5 * (here[0] + north[0])
        face_ref[3, j] = jnp.minimum(here[1], north[1])


def filter_body(leads, sent, scal_ref, pair_hbm, first_ref, second_ref, back_hbm, *refs):
    face_hbm, mine_hbm, send_hbm = refs[:3]
    cur_ref, east_ref, west_ref, north_ref, turn_ref = refs[3:8]
    pair_ref, back_ref, face_ref, out_ref, sems = refs[8:13]
    planes_ref, spare_ref = refs[13:] if leads else (None, None)
    fields, total, tiles, _, _ = cur_ref.shape
    cols = tiles * LANES
    pair = total - 2 * ITERS
    rows = pair // 2
    get_pair = pltpu.make_async_copy(pair_hbm, pair_ref, sems.at[0])
    get_back = pltpu.make_async_copy(back_hbm, back_ref, sems.at[1])
    if leads:
        move_face = pltpu.make_async_copy(face_ref, face_hbm, sems.at[2])
    else:
        move_face = pltpu.make_async_copy(face_hbm, face_ref, sems.at[2])
        move_face.start()
    get_pair.start()
    get_back.start()
    side = scal_ref[0]
    level = (scal_ref[2] + lax.broadcasted_iota(jnp.int32, (GROUP, LANES), 0)).astype(F32)

    def fill(src, dst_row, count):
        for r in range(count):
            for f in range(fields):
                for j in range(tiles):
                    value = src[r * fields + f, :, pl.ds(j * LANES, LANES)]
                    cur_ref[f, dst_row + r, j] = value.astype(F32)
        if leads:
            block = count * PLANES
            for j in range(tiles):
                value = src[pl.ds(count * fields, block // GROUP), :, pl.ds(j * LANES, LANES)]
                planes_ref[j, pl.ds(dst_row * PLANES, block), :] = value.astype(F32).reshape(
                    block, LANES
                )

    @pl.when(scal_ref[1] == 0)
    def _():
        fill(second_ref, 0, ITERS)
        fill(first_ref, ITERS + pair, ITERS)

    @pl.when(scal_ref[1] == 1)
    def _():
        fill(first_ref, 0, ITERS)
        fill(second_ref, ITERS + pair, ITERS)

    if not leads:
        move_face.wait()
    get_pair.wait()
    fill(pair_ref, ITERS, pair)
    if leads:
        make_faces(face_ref, planes_ref, spare_ref)
        move_face.start()

    def weights(r, _):
        for j in range(tiles):

            def spread(i):
                return jnp.broadcast_to(face_ref[i, j, pl.ds(r, 1), :], (GROUP, LANES))

            east = jnp.where(level < spread(1), spread(0), 0.0)
            east_ref[r, j] = east
            north_ref[r, j] = jnp.where(level < spread(3), spread(2), 0.0)
        west_ref[r] = pltpu.roll(east, 1, 1)
        return 0

    lax.fori_loop(0, total, weights, 0, unroll=4)

    def one_field(f, _):
        for step in range(1, ITERS + 1):
            here = [cur_ref[f, step, j] for j in range(tiles)]
            south = [
                north_ref[step - 1, j] * (here[j] - cur_ref[f, step - 1, j]) for j in range(tiles)
            ]
            first = pltpu.roll(here[0], LANES - 1, 1)
            last = pltpu.roll(here[-1], 1, 1)
            for r in range(step, total - step):
                ahead = [cur_ref[f, r + 1, j] for j in range(tiles)]
                flux = west_ref[r] * (here[0] - last)
                for j in range(tiles):
                    beyond = here[j + 1] if j + 1 < tiles else first
                    east = east_ref[r, j] * (beyond - here[j])
                    north = north_ref[r, j] * (ahead[j] - here[j])
                    cur_ref[f, r, j] = here[j] + (east - flux) + (north - south[j])
                    flux = east
                    south[j] = north
                first = pltpu.roll(ahead[0], LANES - 1, 1)
                last = pltpu.roll(ahead[-1], 1, 1)
                here = ahead
        return 0

    lax.fori_loop(0, fields, one_field, 0)

    block = fields * GROUP * rows
    starts = (ITERS + rows * (1 - side), ITERS + rows * side)
    for n, start in enumerate(starts):
        for f in range(fields):
            for r in range(rows):
                for j in range(tiles):
                    spots = pl.ds(n * block + f * GROUP * rows + r, GROUP, stride=rows)
                    turn_ref[j, spots, :] = cur_ref[f, start + r, j]
    get_back.wait()
    flat = jnp.concatenate([turn_ref[j].astype(BF16) for j in range(tiles)], axis=1)
    moved = jnp.dot(flat, back_ref[...], preferred_element_type=F32)
    puts = []
    for n, dst in enumerate((send_hbm, mine_hbm)):
        value = moved[n * block : (n + 1) * block]
        out_ref[n] = value.reshape(fields, GROUP, rows, cols).astype(BF16)
        src = out_ref.at[n]
        if n == 0 and sent < GROUP:
            src = src.at[:, pl.ds(side * (GROUP - sent), sent)]
        puts.append(pltpu.make_async_copy(src, dst, sems.at[3 + n]))
        puts[-1].start()
    for put in puts:
        put.wait()
    if leads:
        move_face.wait()


def filter_rows(scalars, pair, first, second, unspread, faces, fields, rows, sent):
    cols = pair.shape[2]
    total = 2 * rows + 2 * ITERS
    tiles = cols // LANES
    leads = faces is None
    out = jax.ShapeDtypeStruct((fields, GROUP, rows, cols), BF16)
    face = jax.ShapeDtypeStruct((4, tiles, total, LANES), F32)
    scratch = [
        pltpu.VMEM((fields, total, tiles, GROUP, LANES), F32),
        pltpu.VMEM((total, tiles, GROUP, LANES), F32),
        pltpu.VMEM((total, GROUP, LANES), F32),
        pltpu.VMEM((total, tiles, GROUP, LANES), F32),
        pltpu.VMEM((tiles, 2 * fields * GROUP * rows, LANES), F32),
        pltpu.VMEM(pair.shape, BF16),
        pltpu.VMEM((cols, cols), BF16),
        pltpu.VMEM(face.shape, F32),
        pltpu.VMEM((2,) + out.shape, BF16),
        pltpu.SemaphoreType.DMA((5,)),
    ]
    if leads:
        spare = -(-(total + 1) // GROUP) * GROUP
        scratch += [
            pltpu.VMEM((tiles, total * PLANES, LANES), F32),
            pltpu.VMEM((2, tiles, spare, LANES), F32),
        ]

    def body(*refs):
        filter_body(leads, sent, *refs)

    return call(
        body,
        landed=(2, 3),
        out_shape=((face,) if leads else ())
        + (out, jax.ShapeDtypeStruct((fields, sent, rows, cols), BF16)),
        in_specs=[whole(pltpu.SMEM), whole(pl.ANY), whole(), whole(), whole(pl.ANY)]
        + ([] if leads else [whole(pl.ANY)]),
        out_specs=(whole(pl.ANY),) * (3 if leads else 2),
        scratch_shapes=scratch,
        compiler_params=params(24),
        cost_estimate=cost(FILTER_COST),
        name="filter_rows",
    )(scalars, pair, first, second, unspread, *(() if leads else (faces,)))


def project_body(takes, halves, has_start, base_ref, *refs):
    count = len(takes)
    refs = list(refs)
    chunk_refs = refs[:count]
    refs = refs[count:]
    modes_ref = refs.pop(0)
    start_ref = None
    if has_start:
        start_ref = refs.pop(0)
        refs.pop(0)
    out_ref = refs.pop(0)
    keep_ref = give_ref = amp_ref = None
    if halves > 1:
        keep_ref, give_ref = (refs.pop(0), refs.pop(0))
    else:
        amp_ref = refs.pop(0)
    mode_bufs = refs[:count]
    out_sems, mode_sems, chunk_sems = refs[count : count + 3]
    spare = refs[count + 3 :]
    fields, _, rows, cols = chunk_refs[0].shape
    modes = modes_ref.shape[0]
    fetches = [
        pltpu.make_async_copy(
            modes_ref.at[:, pl.ds(base_ref[n, 0], takes[n])], mode_bufs[n], mode_sems.at[n]
        )
        for n in range(count)
    ]
    if has_start:
        chunk_bufs = chunk_refs
        loads = [pltpu.make_async_copy(start_ref, spare[0], chunk_sems.at[0])]
        start_ref = spare[0]
    else:
        chunk_bufs = spare
        loads = [
            pltpu.make_async_copy(chunk_refs[n], chunk_bufs[n], chunk_sems.at[n])
            for n in range(count)
        ]
    copies = [
        pltpu.make_async_copy(
            chunk_bufs[n].at[:, pl.ds(base_ref[n, 1], takes[n])],
            out_ref.at[:, pl.ds(base_ref[n, 0], takes[n])],
            out_sems.at[n],
        )
        for n in range(count)
    ]
    for load in loads:
        load.start()
    if has_start:
        copies[0].start()
    for fetch in fetches:
        fetch.start()
    for n in range(count):
        loads[n].wait()
        if not has_start:
            copies[n].start()
        fetches[n].wait()

        def one_tile(tile, dst, dst_tile, _):
            lanes = pl.ds(pl.multiple_of(tile * LANES, LANES), LANES)
            into = pl.ds(pl.multiple_of(dst_tile * LANES, LANES), LANES)
            sums = []
            for f in range(fields):
                for k in range(modes):
                    if n > 0:
                        sums.append(amp_ref[f, k, :, lanes])
                    elif has_start:
                        sums.append(start_ref[f, k, :, lanes])
                    else:
                        sums.append(jnp.zeros((rows, LANES), F32))
            for i in range(takes[n]):
                values = [
                    chunk_bufs[n][f, base_ref[n, 1] + i, :, lanes].astype(F32)
                    for f in range(fields)
                ]
                for k in range(modes):
                    mode = mode_bufs[n][k, i, :, lanes].astype(F32)
                    for f in range(fields):
                        sums[f * modes + k] = sums[f * modes + k] + mode * values[f]
            for f in range(fields):
                for k in range(modes):
                    dst[f, k, :, into] = sums[f * modes + k]
            return 0

        tiles = cols // LANES
        if halves == 1:
            lax.fori_loop(0, tiles, lambda i, z: one_tile(i, amp_ref, i, z), 0)
        else:
            width = tiles // halves
            mine = base_ref[n, 2] * width
            rest = (1 - base_ref[n, 2]) * width
            lax.fori_loop(0, width, lambda i, z: one_tile(rest + i, give_ref, i, z), 0)
            lax.fori_loop(0, width, lambda i, z: one_tile(mine + i, keep_ref, i, z), 0)
    for copy in copies:
        copy.wait()


def project(bases, chunks, takes, vertical_modes, levels, halves, carried=()):
    count = len(chunks)
    fields, _, rows, cols = chunks[0].shape
    modes = vertical_modes.shape[0]

    def body(*refs):
        project_body(takes, halves, bool(carried), *refs)

    amplitude = jax.ShapeDtypeStruct((fields, modes, rows, cols // halves), F32)

    return call(
        body,
        landed=(1,) if carried else (),
        out_shape=(jax.ShapeDtypeStruct((fields, levels, rows, cols), BF16),)
        + (amplitude,) * halves,
        in_specs=[whole(pltpu.SMEM)]
        + [whole() if carried else whole(pl.ANY)] * count
        + [whole(pl.ANY)]
        + ([whole(pl.ANY), whole(pl.ANY)] if carried else []),
        out_specs=(whole(pl.ANY),) + (whole(),) * halves,
        input_output_aliases={count + 3: 0} if carried else {},
        scratch_shapes=[pltpu.VMEM((modes, take, rows, cols), BF16) for take in takes]
        + [pltpu.SemaphoreType.DMA((count,))] * 3
        + (
            [pltpu.VMEM((fields, modes, rows, cols), F32)]
            if carried
            else [pltpu.VMEM(chunk.shape, BF16) for chunk in chunks]
        ),
        compiler_params=params(24),
        cost_estimate=cost(PROJECT_COST),
        name="project",
    )(bases, *chunks, vertical_modes, *carried)


def flux_body(keep_ref, other_ref, out_ref):
    total = keep_ref[...] + other_ref[...]
    out_ref[0] = total[0] * total[2]
    out_ref[1] = total[1] * total[2]
    out_ref[2] = 0.5 * (total[0] * total[0] + total[1] * total[1])


def statics_planes(diffusivity, depth):
    high = lax.reduce_precision(diffusivity, 8, 7)
    middle = lax.reduce_precision(diffusivity - high, 8, 7)
    low = diffusivity - high - middle
    return jnp.stack([high, middle, low, depth]).astype(BF16)


def per_device(fields, vertical_modes, diffusivity, land_mask, wet_levels):
    count, levels, rows, cols = fields.shape
    size = lax.axis_size("row")
    row = lax.axis_index("row")
    lev = lax.axis_index("lev")
    side = row % 2
    pairs = [(i, i ^ 1) for i in range(size)]
    odd = (row // 2) % 2
    near = [(i, i ^ 2) for i in range(size)]
    far = [(i, ((i + 2) ^ 2) - 2) for i in range(2, size - 2)]
    chunks = -(-(-(-levels // 2)) // GROUP)

    def base(c, which):
        return jnp.where(which == 0, GROUP * c, levels - GROUP * (c + 1)).astype(jnp.int32)

    theirs = [base(c, 1 - side) for c in range(chunks)]
    ours = [base(c, side) for c in range(chunks)]
    depth = (land_mask * wet_levels).astype(F32)
    planes = statics_planes(diffusivity, depth)
    parts = []
    for c, b in enumerate(theirs):
        piece = lax.dynamic_slice_in_dim(fields, b, GROUP, 1)
        piece = piece.reshape(count * GROUP, rows, cols)
        if c == 0:
            piece = jnp.concatenate([piece, planes], axis=0)
        parts.append(lax.ppermute(piece, "row", pairs))
    spread, unspread, statics, *owns = turn(ours, fields, planes)

    cut = levels - (2 * chunks - 1) * GROUP
    skip = jnp.where(side == 0, GROUP - cut, 0).astype(jnp.int32)
    where = jnp.stack([side, odd])
    mine, returned, edges = ([], [], [])
    faces = None
    for c in range(chunks):
        part = parts[c]
        if c > 0:
            part, *_ = lax.optimization_barrier((part, edges[-1]))
        pair, first, second = gather_rows(
            where, owns[c], part, spread, statics if c == 0 else None
        )
        edges.append(first)
        first = lax.ppermute(first, "row", near)
        second = lax.ppermute(second, "row", far)
        if c > 0:
            first, *_ = lax.optimization_barrier((first, mine[-1], returned[: c - 1]))
        sent = GROUP if c + 1 < chunks else cut
        scalars = jnp.stack([side, odd, lev * levels + ours[c]])
        *lead, kept, gone = filter_rows(
            scalars, pair, first, second, unspread, faces, count, rows, sent
        )
        if c == 0:
            faces = lead[0]
        mine.append(kept)
        returned.append(lax.ppermute(gone, "row", pairs))

    zero = jnp.zeros((), jnp.int32)
    bases = [jnp.stack([b, zero]) for b in ours + theirs[:-1]]
    filtered, amplitude = project(
        jnp.stack(bases),
        mine + returned[:-1],
        [GROUP] * (2 * chunks - 1),
        vertical_modes,
        levels,
        1,
    )
    filtered, keep, give = project(
        jnp.stack([theirs[-1] + skip, zero, lev])[None],
        returned[-1:],
        [cut],
        vertical_modes,
        levels,
        lax.axis_size("lev"),
        (amplitude, filtered),
    )
    other = lax.ppermute(give, "lev", [(0, 1), (1, 0)])
    (modal_flux,) = call(
        flux_body,
        landed=(1,),
        out_shape=(jax.ShapeDtypeStruct(keep.shape, F32),),
        in_specs=[whole(), whole()],
        out_specs=(whole(),),
        name="flux",
    )(keep, other)
    return (filtered, modal_flux)


def solution(mesh):
    placed = (
        P("group", "lev", "row", None),
        P(None, "lev", "row", None),
        P("row", None),
        P("row", None),
        P("row", None),
    )
    return jax.shard_map(
        per_device,
        mesh=mesh,
        in_specs=placed,
        out_specs=(P("group", "lev", "row", None), P("group", None, "row", "lev")),
        check_vma=False,
    )
```

```python
import jax
import jax.numpy as jnp
from jax import lax
from jax.experimental import pallas as pl
from jax.experimental.pallas import tpu as pltpu
from jax.sharding import PartitionSpec as P

ITERS = 10
TURN_COST = 20
GATHER_COST = 20
FILTER_COST = 1
PROJECT_COST = 20
GROUP = 8
LANES = 128
PLANES = 4
F32 = jnp.float32
BF16 = jnp.bfloat16


def whole(space=pltpu.VMEM):
    return pl.BlockSpec(memory_space=space)


def call(body, landed=(), **kw):
    shapes = tuple(pltpu.HBM(a.shape, a.dtype) for a in kw.pop("out_shape"))
    inner = pl.pallas_call(body, out_shape=shapes, **kw)

    def run(*args):
        pinned = []
        for i, (arg, spec) in enumerate(zip(args, kw["in_specs"])):
            if spec.memory_space != pltpu.SMEM:
                space = pltpu.VMEM if i in landed else pltpu.HBM
                arg = pltpu.with_memory_space_constraint(arg, space)
            pinned.append(arg)
        return inner(*pinned)

    return run


def params(mib):
    return pltpu.CompilerParams(vmem_limit_bytes=mib * 1024 * 1024)


def cost(us):
    return pl.CostEstimate(flops=us * 1_150_000_000, transcendentals=0, bytes_accessed=us * 3_690_000)


def spread_fill(spread_ref, unspread_ref):
    cols = spread_ref.shape[0]
    tiles = cols // LANES
    for first in range(0, cols, LANES):
        here = first + lax.broadcasted_iota(jnp.int32, (LANES, cols), 0)
        there = lax.broadcasted_iota(jnp.int32, (LANES, cols), 1)
        rows = pl.ds(first, LANES)
        to_spot = here == (there % LANES) * tiles + there // LANES
        to_col = there == (here % LANES) * tiles + here // LANES
        spread_ref[rows, :] = jnp.where(to_spot, 1.0, 0.0).astype(BF16)
        unspread_ref[rows, :] = jnp.where(to_col, 1.0, 0.0).astype(BF16)


def turn_piece(piece, spread_ref, turn_ref, put, put_statics=None):
    count, rows, cols = piece.shape
    flat = piece.astype(F32).reshape(count * rows, cols).astype(BF16)
    moved = jnp.dot(flat, spread_ref[...], preferred_element_type=F32)
    fields = count // GROUP
    for j in range(cols // LANES):
        turn_ref[j, pl.ds(0, count * rows), :] = moved[:, j * LANES : (j + 1) * LANES]
    for j in range(cols // LANES):
        lanes = pl.ds(j * LANES, LANES)
        for r in range(rows):
            for f in range(fields):
                value = turn_ref[j, pl.ds(f * GROUP * rows + r, GROUP, stride=rows), :]
                put(r, f, fields, lanes, value.astype(BF16))
            if put_statics is not None:
                first = fields * GROUP * rows + r
                put_statics(r, lanes, turn_ref[j, pl.ds(first, PLANES, stride=rows), :])


def turn_body(base_ref, fields_ref, planes_ref, spread_ref, unspread_ref, statics_ref, *refs):
    buf_ref, turn_ref, sems = refs[-3:]
    outs = refs[:-3]
    _, fields, _, rows, cols = buf_ref.shape
    copies = [
        pltpu.make_async_copy(
            fields_ref.at[:, pl.ds(base_ref[n], GROUP)], buf_ref.at[n], sems.at[n]
        )
        for n in range(len(outs))
    ]
    for copy in copies:
        copy.start()
    spread_fill(spread_ref, unspread_ref)
    for n, out in enumerate(outs):
        copies[n].wait()

        def put(r, f, count, lanes, value):
            out[r * count + f, :, lanes] = value

        def put_statics(r, lanes, value):
            at = r * PLANES
            statics_ref[at // GROUP, pl.ds(at % GROUP, PLANES), lanes] = value

        piece = buf_ref[n].reshape(fields * GROUP, rows, cols)
        if n == 0:
            piece = jnp.concatenate([piece, planes_ref[...]], axis=0)
        turn_piece(piece, spread_ref, turn_ref, put, put_statics if n == 0 else None)


def turn(bases, fields, planes):
    count, _, rows, cols = fields.shape
    out = jax.ShapeDtypeStruct((rows * count, GROUP, cols), BF16)
    square = jax.ShapeDtypeStruct((cols, cols), BF16)
    many = len(bases)
    return call(
        turn_body,
        out_shape=(square, square, jax.ShapeDtypeStruct((rows * PLANES // GROUP, GROUP, cols), F32))
        + (out,) * many,
        in_specs=[whole(pltpu.SMEM), whole(pl.ANY), whole()],
        out_specs=(whole(),) * (3 + many),
        scratch_shapes=[
            pltpu.VMEM((many, count, GROUP, rows, cols), BF16),
            pltpu.VMEM((cols // LANES, (count * GROUP + PLANES) * rows, LANES), F32),
            pltpu.SemaphoreType.DMA((many,)),
        ],
        compiler_params=params(16),
        cost_estimate=cost(TURN_COST),
        name="turn",
    )(jnp.stack(bases), fields, planes)


def gather_body(where_ref, own_ref, part_ref, spread_ref, *refs):
    refs = list(refs)
    own_statics_ref = refs.pop(0) if len(refs) > 4 else None
    pair_ref, first_ref, second_ref, turn_ref = refs[:4]
    statics_ref = refs[4] if own_statics_ref is not None else None
    rows = part_ref.shape[1]
    fields = own_ref.shape[0] // rows
    side, odd = (where_ref[0], where_ref[1])
    own_start = side * rows
    part_start = rows - own_start
    for r in range(rows * fields):
        pair_ref[own_start * fields + r] = own_ref[r]

    def put(r, f, count, lanes, value):
        pair_ref[(part_start + r) * count + f, :, lanes] = value

    put_statics = None
    if statics_ref is not None:
        tiles = rows * PLANES // GROUP
        statics_ref[pl.ds(side * tiles, tiles)] = own_statics_ref[...]

        def put_statics(r, lanes, value):
            at = r * PLANES
            base = (1 - side) * tiles + at // GROUP
            statics_ref[base, pl.ds(at % GROUP, PLANES), lanes] = value

    turn_piece(part_ref[...], spread_ref, turn_ref, put, put_statics)
    tail = 2 * rows - ITERS
    for dst, pick in ((first_ref, 1 - odd), (second_ref, odd)):
        for r in range(ITERS * fields):
            dst[r] = pair_ref[pick * tail * fields + r]
        if statics_ref is not None:
            count = ITERS * PLANES // GROUP
            value = statics_ref[pl.ds(pick * (tail * PLANES // GROUP), count)]
            dst[pl.ds(ITERS * fields, count)] = value.astype(BF16)
    if statics_ref is not None:
        pair_ref[pl.ds(2 * rows * fields, statics_ref.shape[0])] = statics_ref[...].astype(BF16)


def gather_rows(where, own, part, spread, statics=None):
    count, rows, cols = part.shape
    fields = own.shape[0] // rows
    extra = 0 if statics is None else PLANES

    def out(n):
        return jax.ShapeDtypeStruct((n * fields + n * extra // GROUP, GROUP, cols), BF16)

    scratch = [pltpu.VMEM((cols // LANES, count * rows, LANES), F32)]
    if statics is not None:
        scratch.append(pltpu.VMEM((2 * rows * PLANES // GROUP, GROUP, cols), F32))
    args = (where, own, part, spread) + (() if statics is None else (statics,))
    return call(
        gather_body,
        landed=(2,),
        out_shape=(out(2 * rows), out(ITERS), out(ITERS)),
        in_specs=[whole(pltpu.SMEM)] + [whole()] * (len(args) - 1),
        out_specs=(whole(),) * 3,
        scratch_shapes=scratch,
        compiler_params=params(16),
        cost_estimate=cost(GATHER_COST),
        name="gather_rows",
    )(*args)


def make_faces(face_ref, planes_ref, spare_ref):
    _, tiles, total, _ = face_ref.shape
    spare_ref[...] = jnp.zeros(spare_ref.shape, F32)

    def plane(j, p):
        return planes_ref[j, pl.ds(p, total, stride=PLANES), :]

    for j in range(tiles):
        spare_ref[0, j, pl.ds(0, total), :] = plane(j, 0) + plane(j, 1) + plane(j, 2)
        spare_ref[1, j, pl.ds(0, total), :] = plane(j, 3)
    lane = lax.broadcasted_iota(jnp.int32, (total, LANES), 1)
    for j in range(tiles):
        here, east, north = ([], [], [])
        for i in range(2):
            here.append(spare_ref[i, j, pl.ds(0, total), :])
            if j + 1 < tiles:
                east.append(spare_ref[i, j + 1, pl.ds(0, total), :])
            else:
                east.append(pltpu.roll(spare_ref[i, 0], LANES - 1, 1)[:total])
            north.append(spare_ref[i, j, pl.ds(1, total), :])
        wet_east = jnp.minimum(here[1], east[1])
        if j + 1 == tiles:
            wet_east = jnp.where(lane == LANES - 1, 0.0, wet_east)
        face_ref[0, j] = 0.5 * (here[0] + east[0])
        face_ref[1, j] = wet_east
        face_ref[2, j] = 0.5 * (here[0] + north[0])
        face_ref[3, j] = jnp.minimum(here[1], north[1])


def filter_body(leads, sent, scal_ref, pair_hbm, first_ref, second_ref, back_hbm, *refs):
    face_hbm, mine_hbm, send_hbm = refs[:3]
    cur_ref, east_ref, west_ref, north_ref, turn_ref = refs[3:8]
    pair_ref, back_ref, face_ref, out_ref, sems = refs[8:13]
    planes_ref, spare_ref = refs[13:] if leads else (None, None)
    fields, total, tiles, _, _ = cur_ref.shape
    cols = tiles * LANES
    pair = total - 2 * ITERS
    rows = pair // 2
    get_pair = pltpu.make_async_copy(pair_hbm, pair_ref, sems.at[0])
    get_back = pltpu.make_async_copy(back_hbm, back_ref, sems.at[1])
    if leads:
        move_face = pltpu.make_async_copy(face_ref, face_hbm, sems.at[2])
    else:
        move_face = pltpu.make_async_copy(face_hbm, face_ref, sems.at[2])
        move_face.start()
    get_pair.start()
    get_back.start()
    side = scal_ref[0]
    level = (scal_ref[2] + lax.broadcasted_iota(jnp.int32, (GROUP, LANES), 0)).astype(F32)

    def fill(src, dst_row, count):
        for r in range(count):
            for f in range(fields):
                for j in range(tiles):
                    value = src[r * fields + f, :, pl.ds(j * LANES, LANES)]
                    cur_ref[f, dst_row + r, j] = value.astype(F32)
        if leads:
            block = count * PLANES
            for j in range(tiles):
                value = src[pl.ds(count * fields, block // GROUP), :, pl.ds(j * LANES, LANES)]
                planes_ref[j, pl.ds(dst_row * PLANES, block), :] = value.astype(F32).reshape(
                    block, LANES
                )

    @pl.when(scal_ref[1] == 0)
    def _():
        fill(second_ref, 0, ITERS)
        fill(first_ref, ITERS + pair, ITERS)

    @pl.when(scal_ref[1] == 1)
    def _():
        fill(first_ref, 0, ITERS)
        fill(second_ref, ITERS + pair, ITERS)

    if leads:
        get_pair.wait()
        fill(pair_ref, ITERS, pair)
        make_faces(face_ref, planes_ref, spare_ref)
        move_face.start()
    else:
        move_face.wait()

    def weights(r, _):
        for j in range(tiles):

            def spread(i):
                return jnp.broadcast_to(face_ref[i, j, pl.ds(r, 1), :], (GROUP, LANES))

            east = jnp.where(level < spread(1), spread(0), 0.0)
            east_ref[r, j] = east
            north_ref[r, j] = jnp.where(level < spread(3), spread(2), 0.0)
        west_ref[r] = pltpu.roll(east, 1, 1)
        return 0

    lax.fori_loop(0, total, weights, 0, unroll=4)
    if not leads:
        get_pair.wait()
        fill(pair_ref, ITERS, pair)

    def one_field(f, _):
        for step in range(1, ITERS + 1):
            here = [cur_ref[f, step, j] for j in range(tiles)]
            south = [
                north_ref[step - 1, j] * (here[j] - cur_ref[f, step - 1, j]) for j in range(tiles)
            ]
            first = pltpu.roll(here[0], LANES - 1, 1)
            last = pltpu.roll(here[-1], 1, 1)
            for r in range(step, total - step):
                ahead = [cur_ref[f, r + 1, j] for j in range(tiles)]
                flux = west_ref[r] * (here[0] - last)
                for j in range(tiles):
                    beyond = here[j + 1] if j + 1 < tiles else first
                    east = east_ref[r, j] * (beyond - here[j])
                    north = north_ref[r, j] * (ahead[j] - here[j])
                    cur_ref[f, r, j] = here[j] + (east - flux) + (north - south[j])
                    flux = east
                    south[j] = north
                first = pltpu.roll(ahead[0], LANES - 1, 1)
                last = pltpu.roll(ahead[-1], 1, 1)
                here = ahead
        return 0

    lax.fori_loop(0, fields, one_field, 0)

    block = fields * GROUP * rows
    starts = (ITERS + rows * (1 - side), ITERS + rows * side)
    for n, start in enumerate(starts):
        for f in range(fields):
            for r in range(rows):
                for j in range(tiles):
                    spots = pl.ds(n * block + f * GROUP * rows + r, GROUP, stride=rows)
                    turn_ref[j, spots, :] = cur_ref[f, start + r, j]
    get_back.wait()
    flat = jnp.concatenate([turn_ref[j].astype(BF16) for j in range(tiles)], axis=1)
    moved = jnp.dot(flat, back_ref[...], preferred_element_type=F32)
    puts = []
    for n, dst in enumerate((send_hbm, mine_hbm)):
        value = moved[n * block : (n + 1) * block]
        out_ref[n] = value.reshape(fields, GROUP, rows, cols).astype(BF16)
        src = out_ref.at[n]
        if n == 0 and sent < GROUP:
            src = src.at[:, pl.ds(side * (GROUP - sent), sent)]
        puts.append(pltpu.make_async_copy(src, dst, sems.at[3 + n]))
        puts[-1].start()
    for put in puts:
        put.wait()
    if leads:
        move_face.wait()


def filter_rows(scalars, pair, first, second, unspread, faces, fields, rows, sent):
    cols = pair.shape[2]
    total = 2 * rows + 2 * ITERS
    tiles = cols // LANES
    leads = faces is None
    out = jax.ShapeDtypeStruct((fields, GROUP, rows, cols), BF16)
    face = jax.ShapeDtypeStruct((4, tiles, total, LANES), F32)
    scratch = [
        pltpu.VMEM((fields, total, tiles, GROUP, LANES), F32),
        pltpu.VMEM((total, tiles, GROUP, LANES), F32),
        pltpu.VMEM((total, GROUP, LANES), F32),
        pltpu.VMEM((total, tiles, GROUP, LANES), F32),
        pltpu.VMEM((tiles, 2 * fields * GROUP * rows, LANES), F32),
        pltpu.VMEM(pair.shape, BF16),
        pltpu.VMEM((cols, cols), BF16),
        pltpu.VMEM(face.shape, F32),
        pltpu.VMEM((2,) + out.shape, BF16),
        pltpu.SemaphoreType.DMA((5,)),
    ]
    if leads:
        spare = -(-(total + 1) // GROUP) * GROUP
        scratch += [
            pltpu.VMEM((tiles, total * PLANES, LANES), F32),
            pltpu.VMEM((2, tiles, spare, LANES), F32),
        ]

    def body(*refs):
        filter_body(leads, sent, *refs)

    return call(
        body,
        landed=(2, 3),
        out_shape=((face,) if leads else ())
        + (out, jax.ShapeDtypeStruct((fields, sent, rows, cols), BF16)),
        in_specs=[whole(pltpu.SMEM), whole(pl.ANY), whole(), whole(), whole(pl.ANY)]
        + ([] if leads else [whole(pl.ANY)]),
        out_specs=(whole(pl.ANY),) * (3 if leads else 2),
        scratch_shapes=scratch,
        compiler_params=params(24),
        cost_estimate=cost(FILTER_COST),
        name="filter_rows",
    )(scalars, pair, first, second, unspread, *(() if leads else (faces,)))


def project_body(takes, halves, has_start, base_ref, *refs):
    count = len(takes)
    refs = list(refs)
    chunk_refs = refs[:count]
    refs = refs[count:]
    modes_ref = refs.pop(0)
    start_ref = None
    if has_start:
        start_ref = refs.pop(0)
        refs.pop(0)
    out_ref = refs.pop(0)
    keep_ref = give_ref = amp_ref = None
    if halves > 1:
        keep_ref, give_ref = (refs.pop(0), refs.pop(0))
    else:
        amp_ref = refs.pop(0)
    mode_bufs = refs[:count]
    out_sems, mode_sems, chunk_sems = refs[count : count + 3]
    spare = refs[count + 3 :]
    fields, _, rows, cols = chunk_refs[0].shape
    modes = modes_ref.shape[0]
    fetches = [
        pltpu.make_async_copy(
            modes_ref.at[:, pl.ds(base_ref[n, 0], takes[n])], mode_bufs[n], mode_sems.at[n]
        )
        for n in range(count)
    ]
    if has_start:
        chunk_bufs = chunk_refs
        loads = [pltpu.make_async_copy(start_ref, spare[0], chunk_sems.at[0])]
        start_ref = spare[0]
    else:
        chunk_bufs = list(spare) + chunk_refs[-1:]
        loads = [
            pltpu.make_async_copy(chunk_refs[n], chunk_bufs[n], chunk_sems.at[n])
            for n in range(count - 1)
        ]
    copies = [
        pltpu.make_async_copy(
            chunk_bufs[n].at[:, pl.ds(base_ref[n, 1], takes[n])],
            out_ref.at[:, pl.ds(base_ref[n, 0], takes[n])],
            out_sems.at[n],
        )
        for n in range(count)
    ]
    for load in loads:
        load.start()
    if has_start:
        copies[0].start()
    for fetch in fetches:
        fetch.start()
    for n in range(count):
        if n < len(loads):
            loads[n].wait()
        if not has_start:
            copies[n].start()
        fetches[n].wait()

        def one_tile(tile, dst, dst_tile, _):
            lanes = pl.ds(pl.multiple_of(tile * LANES, LANES), LANES)
            into = pl.ds(pl.multiple_of(dst_tile * LANES, LANES), LANES)
            sums = []
            for f in range(fields):
                for k in range(modes):
                    if n > 0:
                        sums.append(amp_ref[f, k, :, lanes])
                    elif has_start:
                        sums.append(start_ref[f, k, :, lanes])
                    else:
                        sums.append(jnp.zeros((rows, LANES), F32))
            for i in range(takes[n]):
                values = [
                    chunk_bufs[n][f, base_ref[n, 1] + i, :, lanes].astype(F32)
                    for f in range(fields)
                ]
                for k in range(modes):
                    mode = mode_bufs[n][k, i, :, lanes].astype(F32)
                    for f in range(fields):
                        sums[f * modes + k] = sums[f * modes + k] + mode * values[f]
            for f in range(fields):
                for k in range(modes):
                    dst[f, k, :, into] = sums[f * modes + k]
            return 0

        tiles = cols // LANES
        if halves == 1:
            lax.fori_loop(0, tiles, lambda i, z: one_tile(i, amp_ref, i, z), 0)
        else:
            width = tiles // halves
            mine = base_ref[n, 2] * width
            rest = (1 - base_ref[n, 2]) * width
            lax.fori_loop(0, width, lambda i, z: one_tile(rest + i, give_ref, i, z), 0)
            lax.fori_loop(0, width, lambda i, z: one_tile(mine + i, keep_ref, i, z), 0)
    for copy in copies:
        copy.wait()


def project(bases, chunks, takes, vertical_modes, levels, halves, carried=()):
    count = len(chunks)
    fields, _, rows, cols = chunks[0].shape
    modes = vertical_modes.shape[0]

    def body(*refs):
        project_body(takes, halves, bool(carried), *refs)

    amplitude = jax.ShapeDtypeStruct((fields, modes, rows, cols // halves), F32)

    return call(
        body,
        landed=(count,),
        out_shape=(jax.ShapeDtypeStruct((fields, levels, rows, cols), BF16),)
        + (amplitude,) * halves,
        in_specs=[whole(pltpu.SMEM)]
        + [whole(pl.ANY)] * (count - 1)
        + [whole()]
        + [whole(pl.ANY)]
        + ([whole(pl.ANY), whole(pl.ANY)] if carried else []),
        out_specs=(whole(pl.ANY),) + (whole(),) * halves,
        input_output_aliases={count + 3: 0} if carried else {},
        scratch_shapes=[pltpu.VMEM((modes, take, rows, cols), BF16) for take in takes]
        + [pltpu.SemaphoreType.DMA((count,))] * 3
        + (
            [pltpu.VMEM((fields, modes, rows, cols), F32)]
            if carried
            else [pltpu.VMEM(chunk.shape, BF16) for chunk in chunks[:-1]]
        ),
        compiler_params=params(24),
        cost_estimate=cost(PROJECT_COST),
        name="project",
    )(bases, *chunks, vertical_modes, *carried)


def flux_body(keep_ref, other_ref, out_ref):
    total = keep_ref[...] + other_ref[...]
    out_ref[0] = total[0] * total[2]
    out_ref[1] = total[1] * total[2]
    out_ref[2] = 0.5 * (total[0] * total[0] + total[1] * total[1])


def statics_planes(diffusivity, depth):
    high = lax.reduce_precision(diffusivity, 8, 7)
    middle = lax.reduce_precision(diffusivity - high, 8, 7)
    low = diffusivity - high - middle
    return jnp.stack([high, middle, low, depth]).astype(BF16)


def per_device(fields, vertical_modes, diffusivity, land_mask, wet_levels):
    count, levels, rows, cols = fields.shape
    size = lax.axis_size("row")
    row = lax.axis_index("row")
    lev = lax.axis_index("lev")
    side = row % 2
    pairs = [(i, i ^ 1) for i in range(size)]
    odd = (row // 2) % 2
    near = [(i, i ^ 2) for i in range(size)]
    far = [(i, ((i + 2) ^ 2) - 2) for i in range(2, size - 2)]
    chunks = -(-(-(-levels // 2)) // GROUP)

    def base(c, which):
        return jnp.where(which == 0, GROUP * c, levels - GROUP * (c + 1)).astype(jnp.int32)

    theirs = [base(c, 1 - side) for c in range(chunks)]
    ours = [base(c, side) for c in range(chunks)]
    depth = (land_mask * wet_levels).astype(F32)
    planes = statics_planes(diffusivity, depth)
    parts = []
    for c, b in enumerate(theirs):
        piece = lax.dynamic_slice_in_dim(fields, b, GROUP, 1)
        piece = piece.reshape(count * GROUP, rows, cols)
        if c == 0:
            piece = jnp.concatenate([piece, planes], axis=0)
        parts.append(lax.ppermute(piece, "row", pairs))
    spread, unspread, statics, *owns = turn(ours, fields, planes)

    cut = levels - (2 * chunks - 1) * GROUP
    skip = jnp.where(side == 0, GROUP - cut, 0).astype(jnp.int32)
    where = jnp.stack([side, odd])
    mine, returned, edges = ([], [], [])
    faces = None
    for c in range(chunks):
        part = parts[c]
        if c > 0:
            part, *_ = lax.optimization_barrier((part, edges[-1]))
        pair, first, second = gather_rows(
            where, owns[c], part, spread, statics if c == 0 else None
        )
        edges.append(first)
        first = lax.ppermute(first, "row", near)
        second = lax.ppermute(second, "row", far)
        if c > 0:
            first, *_ = lax.optimization_barrier((first, mine[-1], returned[: c - 1]))
        sent = GROUP if c + 1 < chunks else cut
        scalars = jnp.stack([side, odd, lev * levels + ours[c]])
        *lead, kept, gone = filter_rows(
            scalars, pair, first, second, unspread, faces, count, rows, sent
        )
        if c == 0:
            faces = lead[0]
        mine.append(kept)
        returned.append(lax.ppermute(gone, "row", pairs))

    zero = jnp.zeros((), jnp.int32)
    bases = [jnp.stack([b, zero]) for b in ours + theirs[:-1]]
    filtered, amplitude = project(
        jnp.stack(bases),
        mine + returned[:-1],
        [GROUP] * (2 * chunks - 1),
        vertical_modes,
        levels,
        1,
    )
    filtered, keep, give = project(
        jnp.stack([theirs[-1] + skip, zero, lev])[None],
        returned[-1:],
        [cut],
        vertical_modes,
        levels,
        lax.axis_size("lev"),
        (amplitude, filtered),
    )
    other = lax.ppermute(give, "lev", [(0, 1), (1, 0)])
    (modal_flux,) = call(
        flux_body,
        landed=(1,),
        out_shape=(jax.ShapeDtypeStruct(keep.shape, F32),),
        in_specs=[whole(), whole()],
        out_specs=(whole(),),
        name="flux",
    )(keep, other)
    return (filtered, modal_flux)


def solution(mesh):
    placed = (
        P("group", "lev", "row", None),
        P(None, "lev", "row", None),
        P("row", None),
        P("row", None),
        P("row", None),
    )
    return jax.shard_map(
        per_device,
        mesh=mesh,
        in_specs=placed,
        out_specs=(P("group", "lev", "row", None), P("group", None, "row", "lev")),
        check_vma=False,
    )
```
